512 devices in a mesh: expert: 64 (over z, y), tp: 8 (over x, core).
Axes of the slice: x: 4, y: 8, z: 8, core: 2. Of those that a mesh axis runs over, the one named last changes fastest.
Arguments:
- cotangent: bfloat16 [8192, 2048], P('expert'), may hold values from -6 to 6
- gates: float32 [8192, 8], P('expert'), may hold values from 0.05 to 0.6
- expert_ids: int32 [8192, 8], P('expert'), may hold values from 0 to 127, all different within a row; in each aligned block of 128 rows (0 to 127, 128 to 255, ...) at most 12 rows name the same one
- saved_gate: bfloat16 [128, 768, 768], P('expert', 'tp'), may hold values from -6 to 6
- saved_up: bfloat16 [128, 768, 768], P('expert', 'tp'), may hold values from -6 to 6
- w_gate: bfloat16 [128, 768, 2048], P('expert', 'tp'), may hold values from -0.125 to 0.125
- w_up: bfloat16 [128, 768, 2048], P('expert', 'tp'), may hold values from -0.125 to 0.125
- w_down: bfloat16 [128, 768, 2048], P('expert', 'tp'), may hold values from -0.21875 to 0.21875
Outputs:
- token_grad: float32 [8192, 2048], P(('expert', 'tp'))
The draws below stay inside these ranges and needn't reach their ends.
Inputs may be any that keep to these rules, and one draw needn't show every extreme that they name: `expert_ids`: within the 128 tokens of one group, no expert is named by more than 12 route rows, a bound that some block reaches; a token names 8 different experts.
All inputs are finite; a program needn't handle non-finite values.
Results may differ from the reference program's by a relative error of at most 0.0049.
Values may be sent and summed in bfloat16 or wider, within the bound.
A program may use at most 64 MiB of HBM per device.

```python
import math
import jax
import jax.numpy as jnp
import numpy as np
from jax import lax

D = 2048
FF = 768
TOP = 8
TOK_GROUP = 128
EXPERTS = 128
TOKENS = 8192
CAP = 12
N_EXPERT = 64
N_TP = 8


def steps_of(key, dims, pieces, smallest, top_value):
    factor_of, own = 1.0, jax.random.fold_in(key, 6)
    for dim, shards_of in pieces:
        draws = jnp.exp(jax.random.uniform(jax.random.fold_in(own, dim), (shards_of,), jnp.float32, smallest / len(pieces), top_value / len(pieces)))
        factor_of = factor_of * jnp.repeat(draws, dims[dim] // shards_of).reshape([-1 if axis == dim else 1 for axis in range(len(dims))])
    return factor_of


def shared_out(rng, own, number, rows, number_of, top, limit, skew):
    order = jax.random.permutation(rng, number_of)
    heavy_load, common = portions_of(number_of, rows * top, limit, skew, True), portions_of(number_of, rows * top, limit, skew, False)
    places = jnp.arange(number_of)

    def named(sizes, rotation):
        used = int((sizes > 0).sum())
        fixed = max(1, used // 4)
        passed = fixed + (places - fixed + rotation * (used - fixed)) % max(1, number_of - fixed)
        return jnp.zeros((number_of,), jnp.int32).at[order[jnp.where(places < fixed, places, passed)]].set(jnp.asarray(sizes, jnp.int32))

    sizes = jnp.where(number % 4 == 0, named(heavy_load, number // 4), named(common, number - number // 4 - 1))
    mixed = jax.random.permutation(jax.random.fold_in(own, 3), number_of)
    donor, sink = mixed[0:number_of // 2 * 2:2], mixed[1:number_of // 2 * 2:2]
    room = jnp.minimum(sizes[donor] - 1, limit - sizes[sink]) // 2
    room = jnp.where((donor == order[0]) | (sink == order[0]) | (sizes[sink] == 0), 0, jnp.maximum(room, 0))
    passed = jax.random.randint(jax.random.fold_in(own, 4), (number_of // 2,), 0, 1 << 20) % (room + 1)
    sizes = sizes.at[donor].add(-passed).at[sink].add(passed)
    items = jnp.searchsorted(jnp.cumsum(sizes), jnp.arange(rows * top), side="right").astype(jnp.int32)
    table = items.reshape(top, rows).T
    table = table[jax.random.permutation(jax.random.fold_in(own, 1), rows)]
    rotation = jax.random.randint(jax.random.fold_in(own, 2), (rows, 1), 0, top)
    return jnp.take_along_axis(table, (jnp.arange(top)[None, :] + rotation) % top, axis=1)


def portions_of(number_of, total, reach, lean, full):
    weights = [(1 << 20) // math.isqrt(grade ** lean) + 1 for grade in range(1, number_of + 1)]
    largest = reach if full else min(reach, max(-(-total // number_of), total * weights[0] // sum(weights)))
    least = 1 if total - largest >= number_of - 1 else 0
    counts, rest = [largest] + [least] * (number_of - 1), total - largest - least * (number_of - 1)
    while rest > 0:
        candidates = [i for i in range(1, number_of) if counts[i] < largest] or [i for i in range(1, number_of) if counts[i] < reach]
        pool, budget = sum([weights[i] for i in candidates]), rest
        for i in candidates:
            more = min(reach - counts[i], max(1, budget * weights[i] // pool), rest)
            counts[i] = counts[i] + more
            rest = rest - more
    return np.array(counts)


def centred(key, extent, spread, most, split=(), kind=jnp.bfloat16):
    drawn = jax.random.normal(key, extent, jnp.float32) * spread
    if len(split) > 0:
        drawn = steps_of(key, extent, split, -0.22, 0.18) * drawn
    return jnp.clip(drawn, min=-most, max=most).astype(kind)


def setup_inputs(seed: int = 0) -> dict:
    streams_of = jax.random.split(jax.random.key(seed), 9)
    cotangent = centred(streams_of[0], (TOKENS, D), 1.0, 6.0, ((0, 64),))
    gates = jnp.clip(jnp.exp(math.log(0.6) - 2.4849067 * jax.random.uniform(streams_of[1], (TOKENS, TOP), jnp.float32) ** steps_of(streams_of[1], (TOKENS, TOP), ((0, 64),), -0.2, 0.2)), 0.05, 0.6)
    expert_ids_keys = jax.random.split(jax.random.fold_in(streams_of[2], 1), TOKENS // TOK_GROUP)
    expert_ids_turns = jax.random.permutation(jax.random.fold_in(streams_of[2], 3), TOKENS // TOK_GROUP)
    expert_ids = jax.vmap(lambda own, number: shared_out(jax.random.fold_in(streams_of[2], 2), own, number, TOK_GROUP, EXPERTS, TOP, CAP, 2))(expert_ids_keys, expert_ids_turns).reshape((TOKENS, TOP))
    saved_gate = centred(streams_of[3], (EXPERTS, FF, N_EXPERT * CAP), 1.0, 6.0, ((0, 64), (1, 8)))
    saved_up = centred(streams_of[4], (EXPERTS, FF, N_EXPERT * CAP), 1.0, 6.0, ((0, 64), (1, 8)))
    w_gate = centred(streams_of[5], (EXPERTS, FF, D), D ** -0.5, 0.125, ((0, 64), (1, 8)))
    w_up = centred(streams_of[6], (EXPERTS, FF, D), D ** -0.5, 0.125, ((0, 64), (1, 8)))
    w_down = centred(streams_of[7], (EXPERTS, FF, D), FF ** -0.5, 0.21875, ((0, 64), (1, 8)))
    return dict(cotangent=cotangent, gates=gates, expert_ids=expert_ids, saved_gate=saved_gate, saved_up=saved_up, w_gate=w_gate, w_up=w_up, w_down=w_down)


def slot_positions(group_ids):
    one_hot = (group_ids[:, None] == jnp.arange(EXPERTS, dtype=jnp.int32)[None, :]).astype(jnp.int32)
    before = jnp.cumsum(one_hot, axis=0) - one_hot
    return lax.optimization_barrier(jnp.sum(before * one_hot, axis=1)).astype(jnp.int32)

def expert_grad(operands):
    arrived, pre_gate, pre_up, weight_gate, weight_up, weight_down = operands
    hidden_grad = jnp.dot(weight_down, arrived.T, preferred_element_type=jnp.float32)
    gate_value = pre_gate.astype(jnp.float32)
    up_value = pre_up.astype(jnp.float32)
    sigmoid_gate = jax.nn.sigmoid(gate_value)
    up_grad = (hidden_grad * gate_value * sigmoid_gate).astype(jnp.bfloat16)
    gate_grad = (hidden_grad * up_value * sigmoid_gate * (1.0 + gate_value * (1.0 - sigmoid_gate))).astype(jnp.bfloat16)
    shard_width = FF // N_TP
    slot_total = arrived.shape[0]
    gate_split = gate_grad.astype(jnp.float32).reshape(N_TP, shard_width, slot_total)
    up_split = up_grad.astype(jnp.float32).reshape(N_TP, shard_width, slot_total)
    gate_weight_split = weight_gate.astype(jnp.float32).reshape(N_TP, shard_width, D)
    up_weight_split = weight_up.astype(jnp.float32).reshape(N_TP, shard_width, D)
    partial_value = jnp.einsum('tfs,tfd->tsd', gate_split, gate_weight_split) + jnp.einsum('tfs,tfd->tsd', up_split, up_weight_split)
    rounded = lax.optimization_barrier(partial_value.astype(jnp.bfloat16))
    return lax.optimization_barrier(jnp.sum(rounded.astype(jnp.float32), axis=0))

def reference(cotangent, gates, expert_ids, saved_gate, saved_up, w_gate, w_up, w_down):
    route_total = TOKENS * TOP
    group_ids = expert_ids.reshape(N_EXPERT, TOK_GROUP * TOP)
    slot_pos = lax.map(slot_positions, group_ids)
    group_index = jnp.arange(N_EXPERT, dtype=jnp.int32)[:, None]
    target = ((group_ids * N_EXPERT + group_index) * CAP + slot_pos).reshape(route_total).astype(jnp.int32)
    scaled = (gates[:, :, None] * cotangent.astype(jnp.float32)[:, None, :]).astype(jnp.bfloat16).reshape(route_total, D)
    buffer = jnp.zeros((EXPERTS * N_EXPERT * CAP, D), jnp.bfloat16).at[target].set(scaled)
    buffer = buffer.reshape(EXPERTS, N_EXPERT * CAP, D)
    summed = lax.map(expert_grad, (buffer, saved_gate, saved_up, w_gate, w_up, w_down))
    picked = summed.reshape(EXPERTS * N_EXPERT * CAP, D)[target]
    return lax.optimization_barrier(jnp.sum(picked.reshape(TOKENS, TOP, D), axis=1))
```

```python
import jax
import jax.numpy as jnp
from jax import lax
from jax.experimental import pallas as pl
from jax.experimental.pallas import tpu as pltpu
from jax.sharding import PartitionSpec as P

TP = 8
OWNERS = 64
CAP = 12
LOCAL = 2
ROWS = LOCAL * CAP
F32 = jnp.float32
BF16 = jnp.bfloat16


def div12(x):
    return lax.shift_right_logical(x * 5462, 16)


def div24(x):
    return lax.shift_right_logical(x * 2731, 16)


def route_kernel(cot_ref, gates_ref, ids_ref, out_ref, select_ref):
    tokens, top = ids_ref.shape
    experts = OWNERS * LOCAL
    slots = experts * CAP
    lane = lax.broadcasted_iota(jnp.int32, (tokens, experts), 1)
    named = jnp.zeros((tokens, experts), F32)
    weight = jnp.zeros((tokens, experts), F32)
    for k in range(top):
        hit = ids_ref[:, k : k + 1] == lane
        named = jnp.where(hit, 1.0, named)
        weight = jnp.where(hit, gates_ref[:, k : k + 1], weight)
    row = lax.broadcasted_iota(jnp.int32, (tokens, tokens), 0)
    col = lax.broadcasted_iota(jnp.int32, (tokens, tokens), 1)
    lower = jnp.where(col < row, 1.0, 0.0).astype(BF16)
    before = jnp.dot(lower, named.astype(BF16), preferred_element_type=F32)
    place = jnp.where(named > 0.5, before, 64.0).astype(BF16)
    slot = lax.broadcasted_iota(jnp.int32, (slots, experts), 0)
    owner = div12(slot)
    spread = jnp.where(owner == lax.broadcasted_iota(jnp.int32, (slots, experts), 1), 1.0, 0.0)
    nt = (((1,), (1,)), ((), ()))
    place_of = lax.dot_general(spread.astype(BF16), place, nt, preferred_element_type=F32)
    weight_of = lax.dot_general(
        spread, weight, nt, preferred_element_type=F32, precision=lax.Precision.HIGHEST
    )
    want = (slot - owner * CAP).astype(F32)[:, :tokens]
    select = jnp.where(place_of == want, 1.0, 0.0)
    gate = jnp.sum(select * weight_of, axis=1, keepdims=True)
    select = select.astype(BF16)
    select_ref[...] = select
    picked = jnp.dot(select, cot_ref[...], preferred_element_type=F32)
    out_ref[...] = (picked * gate).astype(BF16)


def route(cot, gates, ids):
    tokens = cot.shape[0]
    slots = OWNERS * ROWS
    return pl.pallas_call(
        route_kernel,
        out_shape=(
            jax.ShapeDtypeStruct((slots, cot.shape[1]), BF16),
            jax.ShapeDtypeStruct((slots, tokens), BF16),
        ),
        name="route",
    )(cot, gates, ids)


def expert_kernel(x_ref, sg_ref, su_ref, wg_ref, wu_ref, wd_ref, out_ref):
    parts, block, width = x_ref.shape
    shard = sg_ref.shape[1]
    cols = sg_ref.shape[2]
    nt = (((1,), (1,)), ((), ()))
    tn = (((0,), (0,)), ((), ()))
    hidden = jnp.zeros((LOCAL * shard, block), F32)
    for k in range(parts):
        hidden += lax.dot_general(
            wd_ref[:, k * width : (k + 1) * width], x_ref[k], nt, preferred_element_type=F32
        )
    slot = lax.broadcasted_iota(jnp.int32, (1, block), 1)
    group = div24(slot)
    inner = slot - group * ROWS
    source = lax.broadcasted_iota(jnp.int32, (cols, block), 0)
    gate_rows = []
    up_rows = []
    for e in range(LOCAL):
        place = inner - e * CAP
        wanted = jnp.where((place >= 0) & (place < CAP), group * CAP + place, -1)
        move = jnp.where(source == wanted, 1.0, 0.0).astype(BF16)
        a = jnp.dot(sg_ref[e], move, preferred_element_type=F32)
        u = jnp.dot(su_ref[e], move, preferred_element_type=F32)
        h = hidden[e * shard : (e + 1) * shard]
        s = jax.nn.sigmoid(a)
        up_rows.append((h * a * s).astype(BF16))
        gate_rows.append((h * u * s * (1.0 + a * (1.0 - s))).astype(BF16))
    up = jnp.concatenate(up_rows, axis=0)
    gate = jnp.concatenate(gate_rows, axis=0)
    for k in range(parts):
        w = slice(k * width, (k + 1) * width)
        total = lax.dot_general(gate, wg_ref[:, w], tn, preferred_element_type=F32)
        total += lax.dot_general(up, wu_ref[:, w], tn, preferred_element_type=F32)
        out_ref[k] = total.astype(BF16)


def experts(x, saved_gate, saved_up, w_gate, w_up, w_down):
    parts, slots, width = x.shape
    steps = 2
    block = slots // steps
    local, shard, cols = saved_gate.shape
    flat = (local * shard, parts * width)
    saved = pl.BlockSpec((local, shard, cols // steps), lambda i: (0, 0, i))
    weight = pl.BlockSpec(flat, lambda i: (0, 0))
    moved = pl.BlockSpec((parts, block, width), lambda i: (0, i, 0))
    return pl.pallas_call(
        expert_kernel,
        grid=(steps,),
        in_specs=[moved, saved, saved, weight, weight, weight],
        out_specs=moved,
        out_shape=jax.ShapeDtypeStruct(x.shape, BF16),
        name="experts",
    )(x, saved_gate, saved_up, w_gate.reshape(flat), w_up.reshape(flat), w_down.reshape(flat))


def body(cotangent, gates, expert_ids, saved_gate, saved_up, w_gate, w_up, w_down):
    tokens, features = cotangent.shape
    width = features // TP
    me = lax.axis_index("tp")
    mine = lax.dynamic_slice(cotangent, (0, me * width), (tokens, width))
    outgoing, select = route(mine, gates, expert_ids)
    outgoing = outgoing.reshape(OWNERS, ROWS, width)
    arrived = lax.all_to_all(outgoing, "expert", split_axis=0, concat_axis=0, tiled=True)
    whole = lax.all_gather(arrived.reshape(OWNERS * ROWS, width), "tp", axis=0)
    partial_value = experts(whole, saved_gate, saved_up, w_gate, w_up, w_down)
    summed = lax.psum_scatter(partial_value, "tp", scatter_dimension=0, tiled=False)
    summed = summed.reshape(OWNERS, ROWS, width)
    returned = lax.all_to_all(summed, "expert", split_axis=0, concat_axis=0, tiled=True)
    combined = lax.dot_general(
        select,
        returned.reshape(OWNERS * ROWS, width),
        (((0,), (0,)), ((), ())),
        preferred_element_type=F32,
    )
    return lax.all_to_all(combined, "tp", split_axis=0, concat_axis=1, tiled=True)


def solution(mesh):
    in_specs = (
        P("expert", None),
        P("expert", None),
        P("expert", None),
        P("expert", "tp", None),
        P("expert", "tp", None),
        P("expert", "tp", None),
        P("expert", "tp", None),
        P("expert", "tp", None),
    )
    out_specs = P(("expert", "tp"), None)
    return jax.shard_map(body, mesh=mesh, in_specs=in_specs, out_specs=out_specs, check_vma=False)
```
